32 devices in a mesh: tilt: 8 (over z, y), tile: 4 (over x, core).
Axes of the slice: x: 2, y: 2, z: 4, core: 2. Of those that a mesh axis runs over, the one named last changes fastest.
Arguments:
- images: float32 [16, 1024, 4096], P('tilt', 'tile'), may hold values from -6 to 6
- taps: float32 [9], replicated, may hold values from -3 to 3
- shifts: int32 [16, 2], P('tilt'), may hold values from -4 to 4
- patch_rows: int32 [16, 16], P('tilt'), may hold values from 0 to 1023
- patch_cols: int32 [16, 16], P('tilt'), may hold values from 0 to 4095
- rows_interp: float32 [64, 1024], P(None, 'tile'), may hold values from -0.1875 to 0.1875
- cols_interp: float32 [64, 4096], replicated, may hold values from -0.09375 to 0.09375
Outputs:
- warps: float32 [16, 64, 64], P('tilt', 'tile')
The draws below stay inside these ranges and needn't reach their ends.
Inputs may be any that keep to these rules, and one draw needn't show every extreme that they name: Row and column shifts lie within plus or minus 4. `patch_rows`: patch centres lie inside the image. `patch_cols`: patch centres lie inside the image.
All inputs are finite; a program needn't handle non-finite values.
Results may differ from the reference program's by a relative error of at most 0.0003.
Values sent between devices are 32-bit elements; how exact they have to be, the bound alone decides.
A program may use at most 128 MiB of HBM per device.

```python
import jax
import jax.numpy as jnp
from jax import lax

COLS = 4096
NODES = 64
RAD = 4
SMAX = 4
PATCH_HALF = 256
PASSES = 2
TILTS = 16
ROWS = 1024
PATCHES = 16


def place_ends(values, stream_key, smallest, high):
    dims = values.shape
    spot = [jax.random.randint(jax.random.fold_in(stream_key, axis), (), 0, dims[axis]) for axis in range(len(dims))]
    values = values.at[tuple(spot)].set(smallest)
    longest = dims.index(max(dims))
    spot[longest] = (spot[longest] + 1) % dims[longest]
    return values.at[tuple(spot)].set(high)


def shard_levels(rng, dims, shards, smallest, high):
    gain = 1.0
    for axis_at, parts in shards:
        draws = jax.random.uniform(jax.random.fold_in(jax.random.fold_in(rng, 6), axis_at), (parts,), jnp.float32, smallest / len(shards), high / len(shards))
        gain = gain * jnp.repeat(jnp.exp(draws), dims[axis_at] // parts).reshape((-1,) + (1,) * (len(dims) - 1 - axis_at))
    return gain


def normal_values(key, dims, deviation, bound, cuts=(), held_as=jnp.bfloat16):
    result = deviation * jax.random.normal(key, dims, jnp.float32)
    if cuts:
        result = result * shard_levels(key, dims, cuts, -0.22, 0.18)
    return jnp.clip(result, -bound, bound).astype(held_as)


def setup_inputs(seed: int = 0) -> dict:
    streams_of = jax.random.split(jax.random.key(seed), 8)
    return {
        "images": normal_values(streams_of[0], (TILTS, ROWS, COLS), 1.0, 6.0, ((0, 8), (1, 4)), jnp.float32),
        "taps": normal_values(streams_of[1], (2 * RAD + 1,), 0.35, 3.0, (), jnp.float32),
        "shifts": place_ends(jax.random.randint(streams_of[2], (TILTS, 2), -SMAX, SMAX + 1), jax.random.fold_in(streams_of[2], 1), -SMAX, SMAX).astype(jnp.int32),
        "patch_rows": place_ends(jax.random.randint(streams_of[3], (TILTS, PATCHES), 0, ROWS), jax.random.fold_in(streams_of[3], 1), 0, ROWS - 1).astype(jnp.int32),
        "patch_cols": place_ends(jax.random.randint(streams_of[4], (TILTS, PATCHES), 0, COLS), jax.random.fold_in(streams_of[4], 1), 0, COLS - 1).astype(jnp.int32),
        "rows_interp": normal_values(streams_of[5], (NODES, ROWS), ROWS ** -0.5, 0.1875, ((1, 4),), jnp.float32),
        "cols_interp": normal_values(streams_of[6], (NODES, COLS), COLS ** -0.5, 0.09375, (), jnp.float32),
    }


epsilon = 1e-6


def filter_columns(stack, taps):
    columns = stack.shape[-1]
    padded = jnp.pad(stack, ((0, 0), (RAD, RAD)))
    total = taps[0] * padded[:, 0:columns]
    for offset in range(1, 2 * RAD + 1):
        total = total + taps[offset] * padded[:, offset:offset + columns]
    return total


def filter_rows(stack, taps):
    count = stack.shape[0]
    padded = jnp.pad(stack, ((RAD, RAD), (0, 0)))
    total = taps[0] * padded[0:count, :]
    for offset in range(1, 2 * RAD + 1):
        total = total + taps[offset] * padded[offset:offset + count, :]
    return total


def patch_mask(prow, pcol):
    row_low = jnp.maximum(prow - PATCH_HALF, 0).astype(jnp.int32)
    row_high = (jnp.minimum(prow + PATCH_HALF, ROWS - 1) + 1).astype(jnp.int32)
    col_low = jnp.maximum(pcol - PATCH_HALF, 0).astype(jnp.int32)
    col_high = (jnp.minimum(pcol + PATCH_HALF, COLS - 1) + 1).astype(jnp.int32)
    corner = jnp.zeros((ROWS + 1, COLS + 1), jnp.float32)
    ones = jnp.ones(prow.shape, jnp.float32)
    corner = corner.at[row_low, col_low].add(ones)
    corner = corner.at[row_low, col_high].add(-ones)
    corner = corner.at[row_high, col_low].add(-ones)
    corner = corner.at[row_high, col_high].add(ones)
    counts = jnp.cumsum(jnp.cumsum(corner, axis=0), axis=1)
    return counts[:ROWS, :COLS]


def reference(images, taps, shifts, patch_rows, patch_cols, rows_interp, cols_interp):
    highest = lax.Precision.HIGHEST

    def one_pair(tilt_index):
        next_index = jnp.minimum(tilt_index + 1, TILTS - 1).astype(jnp.int32)
        current = filter_rows(filter_columns(images[tilt_index], taps), taps)
        following = filter_rows(filter_columns(images[next_index], taps), taps)
        padded = jnp.pad(following, ((SMAX, SMAX), (SMAX, SMAX)))
        moved = lax.dynamic_slice(padded, ((SMAX + shifts[tilt_index, 0]).astype(jnp.int32), (SMAX + shifts[tilt_index, 1]).astype(jnp.int32)), (ROWS, COLS))
        differ = moved - current
        side = jnp.pad(current, ((0, 0), (1, 1)))
        slope = 0.5 * (side[:, 2:] - side[:, :-2])
        valid = (tilt_index < TILTS - 1).astype(jnp.float32)
        weights = patch_mask(patch_rows[tilt_index], patch_cols[tilt_index]) * valid
        grid = jnp.zeros((NODES, NODES), jnp.float32)
        field = jnp.zeros((ROWS, COLS), jnp.float32)
        for step in range(PASSES):
            resid = differ + slope * field
            weighted = weights * slope * resid
            grad = jnp.dot(jnp.dot(rows_interp, weighted, precision=highest), cols_interp.T, precision=highest)
            grad_sq = jnp.sum(grad * grad)
            image_dir = jnp.dot(jnp.dot(rows_interp.T, grad, precision=highest), cols_interp, precision=highest)
            along = slope * image_dir
            curv = jnp.sum(weights * along * along)
            alpha = grad_sq / (curv + epsilon)
            grid = grid - alpha * grad
            field = field - alpha * image_dir
        return grid

    grids = lax.map(one_pair, jnp.arange(TILTS, dtype=jnp.int32))
    return jnp.cumsum(grids, axis=0) - grids
```

```python
import functools

import jax
import jax.numpy as jnp
from jax import lax
from jax.experimental import pallas as pl
from jax.experimental.pallas import tpu as pltpu
from jax.sharding import PartitionSpec as P

RAD = 4
SMAX = 4
PATCH_HALF = 256
MARGIN = RAD + SMAX
CHUNK = 64
COLB = 512
PAD = 128
epsilon = 1e-06
F32 = jnp.float32
BF16 = jnp.bfloat16
HI = lax.Precision.HIGHEST


def shifted(value, axis, steps):
    count = lax.axis_size(axis)
    initial, last = (max(0, -steps), min(count, count - steps))
    return lax.ppermute(value, axis, [(source, source + steps) for source in range(initial, last)])


def split_rows(x):
    hi = x.astype(BF16)
    lo = (x - hi.astype(F32)).astype(BF16)
    return jnp.concatenate([hi, lo, hi], axis=0)


def mm(a, b):
    return jnp.dot(a, b, preferred_element_type=F32)


def mm_hi(a, b):
    return lax.dot_general(
        a, b, (((1,), (0,)), ((), ())), precision=HI, preferred_element_type=F32
    )


def mm_hi_t(a, b):
    return lax.dot_general(
        a, b, (((1,), (1,)), ((), ())), precision=HI, preferred_element_type=F32
    )


def filter_strip(x, taps_ref, cols):
    xp = jnp.concatenate([x, jnp.zeros((x.shape[0], PAD), F32)], axis=1)
    width = cols + PAD
    total = taps_ref[RAD] * xp
    for k in range(2 * RAD + 1):
        if k != RAD:
            total = total + taps_ref[k] * pltpu.roll(xp, (RAD - k) % width, 1)
    return total


def band(taps_ref, dy):
    ext = CHUNK + 2 * MARGIN
    y = lax.broadcasted_iota(jnp.int32, (CHUNK, ext), 0)
    j = lax.broadcasted_iota(jnp.int32, (CHUNK, ext), 1)
    d = j - y - (MARGIN - RAD) - dy
    out = jnp.zeros((CHUNK, ext), F32)
    for k in range(2 * RAD + 1):
        out = jnp.where(d == k, taps_ref[k], out)
    return out


def split3(m):
    hi = m.astype(BF16)
    lo = (m - hi.astype(F32)).astype(BF16)
    return hi, lo


def k1(taps_ref, info_ref, prow_ref, pcol_ref, up_ref, main_ref, down_ref, rcat_ref,
       w_ref, w2_ref, left_ref, e_s, f_s, m_s, p_s, cb_s):
    rows, cols = main_ref.shape[1:]
    t = pl.program_id(0)
    band_start = info_ref[0]
    valid = info_ref[2 + 3 * t].astype(F32)
    e_s[0:8, :] = filter_strip(up_ref[0], taps_ref, cols)[:, :cols]
    e_s[rows + 8 : rows + 16, :] = filter_strip(down_ref[0], taps_ref, cols)[:, :cols]

    def strip(i, c):
        r = pl.multiple_of(i * 8, 8)
        e_s[pl.ds(r + 8, 8), :] = filter_strip(main_ref[0, pl.ds(r, 8), :], taps_ref, cols)[:, :cols]
        return c

    lax.fori_loop(0, rows // 8, strip, 0)
    left_ref[...] = jnp.zeros_like(left_ref)
    patches = prow_ref.shape[2]
    xcol = lax.broadcasted_iota(jnp.int32, (patches, cols), 1)
    cb_s[...] = (jnp.abs(xcol - pcol_ref[0]) <= PATCH_HALF).astype(F32).astype(BF16)
    tm_hi, tm_lo = split3(band(taps_ref, 0))

    def chunk(c, carry):
        base = pl.multiple_of(c * CHUNK, CHUNK)
        yrow = band_start + base + lax.broadcasted_iota(jnp.int32, (CHUNK, patches), 0)
        rb = ((jnp.abs(yrow - prow_ref[0]) <= PATCH_HALF).astype(F32) * valid).astype(BF16)
        for b in range(cols // COLB):
            cs = slice(b * COLB, (b + 1) * COLB)
            e = e_s[pl.ds(base, CHUNK + 2 * MARGIN), cs]
            eh, el = split3(e)
            f_s[:, cs] = mm(tm_hi, eh) + (mm(tm_hi, el) + mm(tm_lo, eh))
            m_s[:, cs] = mm(rb, cb_s[:, cs])

        def weigh(i, cc):
            r = pl.multiple_of(i * 8, 8)
            f = f_s[pl.ds(r, 8), :]
            fp = jnp.concatenate([f, jnp.zeros((8, PAD), F32)], axis=1)
            wd = cols + PAD
            gx = 0.5 * (pltpu.roll(fp, wd - 1, 1) - pltpu.roll(fp, 1, 1))[:, :cols]
            w = m_s[pl.ds(r, 8), :] * gx
            ro = pl.multiple_of(base + r, 8)
            w_ref[0, pl.ds(ro, 8), :] = w
            w2_ref[0, pl.ds(ro, 8), :] = w * gx
            p_s[pl.ds(r, 8), :] = w * f
            return cc

        lax.fori_loop(0, CHUNK // 8, weigh, 0)
        rc = rcat_ref[c]
        for b in range(cols // COLB):
            cs = slice(b * COLB, (b + 1) * COLB)
            left_ref[0, :, cs] += mm(rc, split_rows(p_s[:, cs]))
        return carry

    lax.fori_loop(0, rows // CHUNK, chunk, 0)


def k2(taps_ref, info_ref, up_ref, main_ref, down_ref, rcat_ref, w_ref, left_ref, e_s, *, first):
    rows, cols = main_ref.shape[1:]
    t = pl.program_id(0) + first
    band_start = info_ref[0]
    total_rows = info_ref[1]
    dy = info_ref[3 + 3 * t]
    dx = info_ref[4 + 3 * t]
    wd = cols + PAD
    turn = lax.rem(wd - dx, wd)
    x = lax.broadcasted_iota(jnp.int32, (8, cols), 1) + dx
    inside = (x >= 0) & (x < cols)

    def place(v):
        e = pltpu.roll(filter_strip(v, taps_ref, cols), turn, 1)[:, :cols]
        return jnp.where(inside, e, 0.0)

    e_s[0:8, :] = place(up_ref[0])
    e_s[rows + 8 : rows + 16, :] = place(down_ref[0])

    def strip(i, c):
        r = pl.multiple_of(i * 8, 8)
        e_s[pl.ds(r + 8, 8), :] = place(main_ref[0, pl.ds(r, 8), :])
        return c

    lax.fori_loop(0, rows // 8, strip, 0)
    left_ref[...] = jnp.zeros_like(left_ref)
    tm = band(taps_ref, dy)
    yl = lax.broadcasted_iota(jnp.int32, tm.shape, 0) + band_start + dy

    def chunk(c, carry):
        base = pl.multiple_of(c * CHUNK, CHUNK)
        y = yl + base
        tm_hi, tm_lo = split3(jnp.where((y >= 0) & (y < total_rows), tm, 0.0))
        rc = rcat_ref[c]
        for b in range(cols // COLB):
            cs = slice(b * COLB, (b + 1) * COLB)
            eh, el = split3(e_s[pl.ds(base, CHUNK + 2 * MARGIN), cs])
            q = mm(tm_hi, eh) + (mm(tm_hi, el) + mm(tm_lo, eh))
            p = w_ref[0, pl.ds(base, CHUNK), cs] * q
            left_ref[0, :, cs] += mm(rc, split_rows(p))
        return carry

    lax.fori_loop(0, rows // CHUNK, chunk, 0)


def refine(*refs, n, final, sizes):
    if final:
        (lq_ref, lf_ref, w2_ref, c_ref, ccat_ref, rt_ref, rcat_ref, sel_ref, gl_ref, out_ref,
         left_s, cat_s, acc_s, send_s, slots, csend_s, cslots, ssem, rsem, csem, crsem) = refs
    else:
        (lq_ref, lf_ref, w2_ref, c_ref, ccat_ref, rt_ref, rcat_ref, sel_ref, out_ref,
         left_s, cat_s, acc_s, send_s, slots, ssem, rsem) = refs
    tiles, tilts = sizes
    nodes, cols = c_ref.shape
    rows = rt_ref.shape[0]
    me = lax.axis_index("tile")
    place = lax.axis_index("tilt")
    barrier = pltpu.get_barrier_semaphore()
    for d in range(1, tiles):
        pl.semaphore_signal(barrier, inc=1, device_id={"tile": lax.rem(me + d, tiles)})
    waits = tiles - 1
    if final:
        for d in range(1, tilts):
            pl.semaphore_signal(barrier, inc=1, device_id={"tilt": lax.rem(place + d, tilts)})
        waits += tilts - 1
    pl.semaphore_wait(barrier, waits)

    def exchange(rnd):
        copies = []
        for d in range(1, tiles):
            copies.append(pltpu.make_async_remote_copy(
                src_ref=send_s.at[rnd], dst_ref=slots.at[rnd, me],
                send_sem=ssem.at[rnd, d - 1], recv_sem=rsem.at[rnd, d - 1],
                device_id={"tile": lax.rem(me + d, tiles)}))
        for cp in copies:
            cp.start()
        slots[rnd, me] = send_s[rnd]
        for cp in copies:
            cp.wait()
        total = slots[rnd, 0]
        for k in range(1, tiles):
            total = total + slots[rnd, k]
        return total

    def direction(g, w2, apply):
        g3 = mm_hi(mm_hi(rt_ref[...], g), sel_ref[...])
        hi, lo = split3(g3)
        lane = lax.broadcasted_iota(jnp.int32, g3.shape, 1)
        cat_s[...] = jnp.where(lane < 2 * nodes, hi.astype(F32), lo.astype(F32)).astype(BF16)
        acc_s[...] = jnp.zeros_like(acc_s)
        if apply:
            left_s[...] = jnp.zeros_like(left_s)

        def chunk(c, carry):
            base = pl.multiple_of(c * CHUNK, CHUNK)
            gc = cat_s[pl.ds(base, CHUNK), :]
            rc = rcat_ref[c]
            for b in range(cols // COLB):
                cs = slice(b * COLB, (b + 1) * COLB)
                v = mm(gc, ccat_ref[:, cs])
                y = w2_ref[w2, pl.ds(base, CHUNK), cs] * v
                acc_s[...] += y * v
                if apply:
                    left_s[:, cs] += mm(rc, split_rows(y))
            return carry

        lax.fori_loop(0, rows // CHUNK, chunk, 0)
        return jnp.sum(acc_s[...])

    grids = []
    for s in range(n):
        r = 3 * s
        send_s[r] = jnp.zeros_like(send_s[r])
        send_s[r, :nodes, :nodes] = mm_hi_t(lq_ref[s] - lf_ref[s], c_ref[...])
        g1 = exchange(r)[:nodes, :nodes]
        gg1 = jnp.sum(g1 * g1)
        jj1 = direction(g1, s, True)
        send_s[r + 1] = jnp.zeros_like(send_s[r + 1])
        send_s[r + 1, :nodes, :nodes] = mm_hi_t(left_s[...], c_ref[...])
        send_s[r + 1, nodes : nodes + 8, :] = jnp.full((8, send_s.shape[2]), jj1, F32)
        both = exchange(r + 1)
        h1 = both[:nodes, :nodes]
        jj1 = jnp.sum(both[nodes : nodes + 1, 0:1])
        a1 = jnp.full((nodes, nodes), gg1, F32) / jnp.full((nodes, nodes), jj1 + epsilon, F32)
        g2 = g1 - a1 * h1
        gg2 = jnp.sum(g2 * g2)
        jj2 = direction(g2, s, False)
        send_s[r + 2] = jnp.full(send_s.shape[1:], jj2, F32)
        jj2 = jnp.sum(exchange(r + 2)[0:1, 0:1])
        a2 = jnp.full((nodes, nodes), gg2, F32) / jnp.full((nodes, nodes), jj2 + epsilon, F32)
        grids.append(-(a1 * g1) - a2 * g2)
    if not final:
        for s in range(n):
            out_ref[s] = grids[s]
        return
    share = nodes // tiles
    send_rows = csend_s.shape[0]
    row = lax.broadcasted_iota(jnp.int32, (send_rows, nodes), 0) + me * share
    pick = (row == lax.broadcasted_iota(jnp.int32, (send_rows, nodes), 1)).astype(F32)
    run = jnp.zeros((nodes, nodes), F32)
    count = out_ref.shape[0]
    stack = [gl_ref[i] for i in range(count - n)] + grids
    parts = []
    for i in range(count):
        parts.append(mm_hi(pick, run))
        run = run + stack[i]
    csend_s[...] = jnp.zeros_like(csend_s)
    csend_s[:, :nodes] = mm_hi(pick, run)
    copies = []
    for d in range(1, tilts):
        copies.append(pltpu.make_async_remote_copy(
            src_ref=csend_s, dst_ref=cslots.at[place],
            send_sem=csem.at[d - 1], recv_sem=crsem.at[d - 1],
            device_id={"tilt": lax.rem(place + d, tilts)}))
    for cp in copies:
        cp.start()
    cslots[place] = csend_s[...]
    for cp in copies:
        cp.wait()
    before = jnp.zeros((send_rows, 128), F32)
    for k in range(tilts):
        before = before + jnp.where(k < place, cslots[k], 0.0)
    for i in range(count):
        out_ref[i] = (before[:, :nodes] + parts[i])[:share]


def shards(images, taps, shifts, patch_rows, patch_cols, rows_interp, cols_interp):
    tilt_count, rows, cols = images.shape
    tiles, tilts = lax.axis_size("tile"), lax.axis_size("tilt")
    nodes = cols_interp.shape[0]
    patches = patch_rows.shape[1]
    raw_next = shifted(images[0], "tilt", -1)
    low = shifted(images[:, rows - MARGIN :, :], "tile", 1)
    high = shifted(images[:, :MARGIN, :], "tile", -1)
    rim = shifted(jnp.concatenate([low[0], high[0]], axis=0), "tilt", -1)

    t_global = lax.axis_index("tilt") * tilt_count + jnp.arange(tilt_count, dtype=jnp.int32)
    valid = (t_global < tilt_count * tilts - 1).astype(jnp.int32)
    head = jnp.stack([lax.axis_index("tile") * rows, jnp.int32(rows * tiles)]).astype(jnp.int32)
    info = jnp.concatenate([head, jnp.concatenate([valid[:, None], shifts], axis=1).reshape(-1)])

    def halves(x):
        hi = lax.reduce_precision(x, 8, 7)
        return hi.astype(BF16), (x - hi).astype(BF16)

    chunks = rows // CHUNK
    rh, rl = halves(rows_interp.reshape(nodes, chunks, CHUNK).transpose(1, 0, 2))
    rcat = jnp.concatenate([rh, rh, rl], axis=2)
    ch, cl = halves(cols_interp)
    ccat = jnp.concatenate([ch, cl, ch], axis=0)
    eye = jnp.eye(nodes, dtype=F32)
    sel = jnp.concatenate([eye, eye, eye], axis=1)

    smem = pl.BlockSpec(memory_space=pltpu.SMEM)
    vmem = pl.BlockSpec(memory_space=pltpu.VMEM)
    vm = 60 << 20

    def per(shape, off=0):
        return pl.BlockSpec((1,) + shape, lambda i: (i + off, 0, 0))

    def whole(shape):
        return pl.BlockSpec(shape, lambda i: (0,) * len(shape))

    e_scratch = pltpu.VMEM((rows + 2 * MARGIN, cols), F32)
    big = rows * cols
    w, w2, left_f = pl.pallas_call(
        k1,
        grid=(tilt_count,),
        in_specs=[smem, smem, per((1, patches)), per((patches, 1)), per((MARGIN, cols)),
                  per((rows, cols)), per((MARGIN, cols)), whole(rcat.shape)],
        out_specs=[per((rows, cols)), per((rows, cols)), per((nodes, cols))],
        out_shape=[jax.ShapeDtypeStruct((tilt_count, rows, cols), F32),
                   jax.ShapeDtypeStruct((tilt_count, rows, cols), F32),
                   jax.ShapeDtypeStruct((tilt_count, nodes, cols), F32)],
        scratch_shapes=[e_scratch, pltpu.VMEM((CHUNK, cols), F32), pltpu.VMEM((CHUNK, cols), F32),
                        pltpu.VMEM((CHUNK, cols), F32), pltpu.VMEM((patches, cols), BF16)],
        compiler_params=pltpu.CompilerParams(vmem_limit_bytes=vm),
        cost_estimate=pl.CostEstimate(flops=60 * big * tilt_count, bytes_accessed=40 * big * tilt_count,
                                      transcendentals=0),
        name="weigh",
    )(taps, info, patch_rows[:, None, :], patch_cols[:, :, None], low, images, high, rcat)

    def partner(up, main, down, first, count, off):
        return pl.pallas_call(
            functools.partial(k2, first=first),
            grid=(count,),
            in_specs=[smem, smem, per((MARGIN, cols), off), per((rows, cols), off),
                      per((MARGIN, cols), off), whole(rcat.shape), per((rows, cols), first)],
            out_specs=per((nodes, cols)),
            out_shape=jax.ShapeDtypeStruct((count, nodes, cols), F32),
            scratch_shapes=[e_scratch],
            compiler_params=pltpu.CompilerParams(vmem_limit_bytes=vm),
            cost_estimate=pl.CostEstimate(flops=40 * big * count, bytes_accessed=30 * big * count,
                                          transcendentals=0),
            name="partner",
        )(taps, info, up, main, down, rcat, w)

    rt = rows_interp.T

    def step(lq, lf, w2s, final, cid, extra=()):
        n = lq.shape[0]
        scratch = [pltpu.VMEM((nodes, cols), F32), pltpu.VMEM((rows, 3 * nodes), BF16),
                   pltpu.VMEM((CHUNK, COLB), F32), pltpu.VMEM((3 * n, nodes + 8, 128), F32),
                   pltpu.VMEM((3 * n, tiles, nodes + 8, 128), F32)]
        sems = [pltpu.SemaphoreType.DMA((3 * n, tiles - 1)), pltpu.SemaphoreType.DMA((3 * n, tiles - 1))]
        if final:
            share = nodes // tiles
            wide = max(8, share)
            scratch += [pltpu.VMEM((wide, 128), F32), pltpu.VMEM((tilts, wide, 128), F32)]
            sems += [pltpu.SemaphoreType.DMA((tilts - 1,)), pltpu.SemaphoreType.DMA((tilts - 1,))]
            out = jax.ShapeDtypeStruct((tilt_count, share, nodes), F32)
        else:
            out = jax.ShapeDtypeStruct((n, nodes, nodes), F32)
        off = tilt_count - 1 if final else 0
        args = (lq, lf, w2s, cols_interp, ccat, rt, rcat, sel) + tuple(extra)
        specs = [whole(lq.shape), pl.BlockSpec((n,) + lf.shape[1:], lambda i: (off, 0, 0)),
                 pl.BlockSpec((n,) + w2s.shape[1:], lambda i: (off, 0, 0))]
        specs += [whole(a.shape) for a in args[3:]]
        return pl.pallas_call(
            functools.partial(refine, n=n, final=final, sizes=(tiles, tilts)),
            grid=(1,),
            in_specs=specs,
            out_specs=pl.BlockSpec(out.shape, lambda i: (0, 0, 0)),
            out_shape=out,
            scratch_shapes=scratch + sems,
            compiler_params=pltpu.CompilerParams(
                collective_id=cid, has_side_effects=True, vmem_limit_bytes=vm),
            cost_estimate=pl.CostEstimate(flops=60 * big, bytes_accessed=40 * big, transcendentals=0),
            name="refine_last" if final else "refine_local",
        )(*args)

    local = tilt_count - 1
    extra = ()
    if local:
        lq = partner(low, images, high, 0, local, 1)
        extra = (step(lq, left_f, w2, False, 1),)
    else:
        extra = (jnp.zeros((1, nodes, nodes), F32),)
    lq_last = partner(rim[None, :MARGIN], raw_next[None], rim[None, MARGIN:], tilt_count - 1, 1, 0)
    return step(lq_last, left_f, w2, True, 2, extra)


def solution(mesh):
    return jax.shard_map(
        shards,
        mesh=mesh,
        in_specs=(
            P("tilt", "tile", None),
            P(),
            P("tilt", None),
            P("tilt", None),
            P("tilt", None),
            P(None, "tile"),
            P(),
        ),
        out_specs=P("tilt", "tile", None),
        check_vma=False,
    )
```

```python
import functools

import jax
import jax.numpy as jnp
from jax import lax
from jax.experimental import pallas as pl
from jax.experimental.pallas import tpu as pltpu
from jax.sharding import PartitionSpec as P

RAD = 4
SMAX = 4
PATCH_HALF = 256
MARGIN = RAD + SMAX
CHUNK = 64
COLB = 512
WIDE = 256
GROUP = 32
PAD = 128
epsilon = 1e-06
F32 = jnp.float32
BF16 = jnp.bfloat16
HI = lax.Precision.HIGHEST


def shifted(value, axis, steps):
    count = lax.axis_size(axis)
    initial, last = (max(0, -steps), min(count, count - steps))
    return lax.ppermute(value, axis, [(source, source + steps) for source in range(initial, last)])


def split_rows(x):
    hi = x.astype(BF16)
    lo = (x - hi.astype(F32)).astype(BF16)
    return jnp.concatenate([hi, lo, hi], axis=0)


def mm(a, b):
    return jnp.dot(a, b, preferred_element_type=F32)


def mm_hi(a, b):
    return lax.dot_general(
        a, b, (((1,), (0,)), ((), ())), precision=HI, preferred_element_type=F32
    )


def mm_hi_t(a, b):
    return lax.dot_general(
        a, b, (((1,), (1,)), ((), ())), precision=HI, preferred_element_type=F32
    )


def toeplitz(taps_ref, dx, th_s, tl_s):
    i = lax.broadcasted_iota(jnp.int32, (2 * WIDE, WIDE), 0)
    o = lax.broadcasted_iota(jnp.int32, (2 * WIDE, WIDE), 1)
    rel = jnp.where(i < WIDE, i, jnp.where(i < WIDE + PAD, i - WIDE - PAD, i - PAD))
    d = rel - o - dx + RAD
    t = jnp.zeros((2 * WIDE, WIDE), F32)
    for k in range(2 * RAD + 1):
        t = jnp.where(d == k, taps_ref[k], t)
    th_s[...], tl_s[...] = split3(t)


def filter_group(load, store, rows, cols, dx, th_s, tl_s):
    blocks = cols // PAD
    zero = jnp.zeros((rows, PAD), BF16)
    his, los = [zero], [zero]
    for b in range(blocks):
        hi, lo = split3(load(b * PAD, PAD))
        his.append(hi)
        los.append(lo)
    his.append(zero)
    los.append(zero)

    def gather(v):
        return jnp.concatenate(
            [jnp.concatenate([v[2 * b + 1], v[2 * b + 2], v[2 * b], v[2 * b + 3]], axis=1)
             for b in range(blocks // 2)], axis=0)

    xh, xl = gather(his), gather(los)
    th = th_s[...]
    e = mm(xh, th) + (mm(xl, th) + mm(xh, tl_s[...]))
    for b in range(blocks // 2):
        v = e[b * rows : (b + 1) * rows]
        if b == 0 or b == blocks // 2 - 1:
            x = lax.broadcasted_iota(jnp.int32, v.shape, 1) + (b * WIDE + dx)
            v = jnp.where((x >= 0) & (x < cols), v, 0.0)
        store(b * WIDE, v)


def filter_pieces(pieces, e_s, cols, dx, th_s, tl_s):
    at = 0
    for ref in pieces:
        m = ref.shape[1]
        groups = m // GROUP

        def body(i, carry, ref=ref, at=at):
            r = pl.multiple_of(i * GROUP, 8)
            ro = pl.multiple_of(i * GROUP + at, 8)

            def load(c, w):
                return ref[0, pl.ds(r, GROUP), c : c + w]

            def store(c, v):
                e_s[pl.ds(ro, GROUP), c : c + WIDE] = v

            filter_group(load, store, GROUP, cols, dx, th_s, tl_s)
            return carry

        if groups:
            lax.fori_loop(0, groups, body, 0)
        done = groups * GROUP
        left = m - done
        while left:
            size = 16 if left >= 16 else 8

            def load(c, w, ref=ref, done=done, size=size):
                return ref[0, done : done + size, c : c + w]

            def store(c, v, at=at, done=done, size=size):
                e_s[at + done : at + done + size, c : c + WIDE] = v

            filter_group(load, store, size, cols, dx, th_s, tl_s)
            done += size
            left -= size
        at += m


def band(taps_ref, dy):
    ext = CHUNK + 2 * MARGIN
    y = lax.broadcasted_iota(jnp.int32, (CHUNK, ext), 0)
    j = lax.broadcasted_iota(jnp.int32, (CHUNK, ext), 1)
    d = j - y - (MARGIN - RAD) - dy
    out = jnp.zeros((CHUNK, ext), F32)
    for k in range(2 * RAD + 1):
        out = jnp.where(d == k, taps_ref[k], out)
    return out


def split3(m):
    hi = m.astype(BF16)
    lo = (m - hi.astype(F32)).astype(BF16)
    return hi, lo


def k1(taps_ref, info_ref, prow_ref, pcol_ref, up_ref, main_ref, down_ref, rcat_ref,
       w_ref, w2_ref, left_ref, e_s, f_s, m_s, p_s, cb_s, th_s, tl_s):
    rows, cols = main_ref.shape[1:]
    t = pl.program_id(0)
    band_start = info_ref[0]
    valid = info_ref[2 + 3 * t].astype(F32)
    toeplitz(taps_ref, 0, th_s, tl_s)
    filter_pieces((up_ref, main_ref, down_ref), e_s, cols, 0, th_s, tl_s)
    left_ref[...] = jnp.zeros_like(left_ref)
    patches = prow_ref.shape[2]
    xcol = lax.broadcasted_iota(jnp.int32, (patches, cols), 1)
    cb_s[...] = (jnp.abs(xcol - pcol_ref[0]) <= PATCH_HALF).astype(F32).astype(BF16)
    tm_hi, tm_lo = split3(band(taps_ref, 0))

    def chunk(c, carry):
        base = pl.multiple_of(c * CHUNK, CHUNK)
        yrow = band_start + base + lax.broadcasted_iota(jnp.int32, (CHUNK, patches), 0)
        rb = ((jnp.abs(yrow - prow_ref[0]) <= PATCH_HALF).astype(F32) * valid).astype(BF16)
        for b in range(cols // COLB):
            cs = slice(b * COLB, (b + 1) * COLB)
            e = e_s[pl.ds(base, CHUNK + 2 * MARGIN), cs]
            eh, el = split3(e)
            f_s[:, cs] = mm(tm_hi, eh) + (mm(tm_hi, el) + mm(tm_lo, eh))
            m_s[:, cs] = mm(rb, cb_s[:, cs])

        def weigh(i, cc):
            r = pl.multiple_of(i * 8, 8)
            f = f_s[pl.ds(r, 8), :]
            fp = jnp.concatenate([f, jnp.zeros((8, PAD), F32)], axis=1)
            wd = cols + PAD
            gx = 0.5 * (pltpu.roll(fp, wd - 1, 1) - pltpu.roll(fp, 1, 1))[:, :cols]
            w = m_s[pl.ds(r, 8), :] * gx
            ro = pl.multiple_of(base + r, 8)
            w_ref[0, pl.ds(ro, 8), :] = w
            w2_ref[0, pl.ds(ro, 8), :] = w * gx
            p_s[pl.ds(r, 8), :] = w * f
            return cc

        lax.fori_loop(0, CHUNK // 8, weigh, 0)
        rc = rcat_ref[c]
        for b in range(cols // COLB):
            cs = slice(b * COLB, (b + 1) * COLB)
            left_ref[0, :, cs] += mm(rc, split_rows(p_s[:, cs]))
        return carry

    lax.fori_loop(0, rows // CHUNK, chunk, 0)


def k2(taps_ref, info_ref, *refs, first, pieces, start):
    piece_refs = refs[:pieces]
    rcat_ref, w_ref, left_ref, e_s, th_s, tl_s = refs[pieces:]
    rows = sum(p.shape[1] for p in piece_refs) - 2 * MARGIN
    cols = w_ref.shape[2]
    t = pl.program_id(0) + first
    band_start = info_ref[0] + start
    total_rows = info_ref[1]
    dy = info_ref[3 + 3 * t]
    dx = info_ref[4 + 3 * t]
    toeplitz(taps_ref, dx, th_s, tl_s)
    filter_pieces(piece_refs, e_s, cols, dx, th_s, tl_s)
    left_ref[...] = jnp.zeros_like(left_ref)
    tm = band(taps_ref, dy)
    yl = lax.broadcasted_iota(jnp.int32, tm.shape, 0) + band_start + dy

    def chunk(c, carry):
        base = pl.multiple_of(c * CHUNK, CHUNK)
        y = yl + base
        tm_hi, tm_lo = split3(jnp.where((y >= 0) & (y < total_rows), tm, 0.0))
        rc = rcat_ref[c + start // CHUNK]
        for b in range(cols // COLB):
            cs = slice(b * COLB, (b + 1) * COLB)
            eh, el = split3(e_s[pl.ds(base, CHUNK + 2 * MARGIN), cs])
            q = mm(tm_hi, eh) + (mm(tm_hi, el) + mm(tm_lo, eh))
            p = w_ref[0, pl.ds(pl.multiple_of(base + start, CHUNK), CHUNK), cs] * q
            left_ref[0, :, cs] += mm(rc, split_rows(p))
        return carry

    lax.fori_loop(0, rows // CHUNK, chunk, 0)


def refine(*refs, n, final, sizes):
    if final:
        (lq_ref, lf_ref, w2_ref, c_ref, ccat_ref, rt_ref, rcat_ref, sel_ref, gl_ref, out_ref,
         left_s, cat_s, acc_s, send_s, slots, csend_s, cslots, ssem, rsem, csem, crsem) = refs
    else:
        (lq_ref, lf_ref, w2_ref, c_ref, ccat_ref, rt_ref, rcat_ref, sel_ref, out_ref,
         left_s, cat_s, acc_s, send_s, slots, ssem, rsem) = refs
    tiles, tilts = sizes
    nodes, cols = c_ref.shape
    rows = rt_ref.shape[0]
    me = lax.axis_index("tile")
    place = lax.axis_index("tilt")
    barrier = pltpu.get_barrier_semaphore()
    for d in range(1, tiles):
        pl.semaphore_signal(barrier, inc=1, device_id={"tile": lax.rem(me + d, tiles)})
    waits = tiles - 1
    if final:
        for d in range(1, tilts):
            pl.semaphore_signal(barrier, inc=1, device_id={"tilt": lax.rem(place + d, tilts)})
        waits += tilts - 1
    pl.semaphore_wait(barrier, waits)

    def exchange(rnd):
        copies = []
        for d in range(1, tiles):
            copies.append(pltpu.make_async_remote_copy(
                src_ref=send_s.at[rnd], dst_ref=slots.at[rnd, me],
                send_sem=ssem.at[rnd, d - 1], recv_sem=rsem.at[rnd, d - 1],
                device_id={"tile": lax.rem(me + d, tiles)}))
        for cp in copies:
            cp.start()
        slots[rnd, me] = send_s[rnd]
        for cp in copies:
            cp.wait()
        total = slots[rnd, 0]
        for k in range(1, tiles):
            total = total + slots[rnd, k]
        return total

    def direction(g, w2, apply):
        g3 = mm_hi(mm_hi(rt_ref[...], g), sel_ref[...])
        hi, lo = split3(g3)
        lane = lax.broadcasted_iota(jnp.int32, g3.shape, 1)
        cat_s[...] = jnp.where(lane < 2 * nodes, hi.astype(F32), lo.astype(F32)).astype(BF16)
        acc_s[...] = jnp.zeros_like(acc_s)
        if apply:
            left_s[...] = jnp.zeros_like(left_s)

        def chunk(c, carry):
            base = pl.multiple_of(c * CHUNK, CHUNK)
            gc = cat_s[pl.ds(base, CHUNK), :]
            rc = rcat_ref[c]
            for b in range(cols // COLB):
                cs = slice(b * COLB, (b + 1) * COLB)
                v = mm(gc, ccat_ref[:, cs])
                y = w2_ref[w2, pl.ds(base, CHUNK), cs] * v
                acc_s[...] += y * v
                if apply:
                    left_s[:, cs] += mm(rc, split_rows(y))
            return carry

        lax.fori_loop(0, rows // CHUNK, chunk, 0)
        return jnp.sum(acc_s[...])

    grids = []
    for s in range(n):
        r = 3 * s
        send_s[r] = jnp.zeros_like(send_s[r])
        send_s[r, :nodes, :nodes] = mm_hi_t(lq_ref[s] - lf_ref[s], c_ref[...])
        g1 = exchange(r)[:nodes, :nodes]
        gg1 = jnp.sum(g1 * g1)
        jj1 = direction(g1, s, True)
        send_s[r + 1] = jnp.zeros_like(send_s[r + 1])
        send_s[r + 1, :nodes, :nodes] = mm_hi_t(left_s[...], c_ref[...])
        send_s[r + 1, nodes : nodes + 8, :] = jnp.full((8, send_s.shape[2]), jj1, F32)
        both = exchange(r + 1)
        h1 = both[:nodes, :nodes]
        jj1 = jnp.sum(both[nodes : nodes + 1, 0:1])
        a1 = jnp.full((nodes, nodes), gg1, F32) / jnp.full((nodes, nodes), jj1 + epsilon, F32)
        g2 = g1 - a1 * h1
        gg2 = jnp.sum(g2 * g2)
        jj2 = direction(g2, s, False)
        send_s[r + 2] = jnp.full(send_s.shape[1:], jj2, F32)
        jj2 = jnp.sum(exchange(r + 2)[0:1, 0:1])
        a2 = jnp.full((nodes, nodes), gg2, F32) / jnp.full((nodes, nodes), jj2 + epsilon, F32)
        grids.append(-(a1 * g1) - a2 * g2)
    if not final:
        for s in range(n):
            out_ref[s] = grids[s]
        return
    share = nodes // tiles
    send_rows = csend_s.shape[0]
    row = lax.broadcasted_iota(jnp.int32, (send_rows, nodes), 0) + me * share
    pick = (row == lax.broadcasted_iota(jnp.int32, (send_rows, nodes), 1)).astype(F32)
    run = jnp.zeros((nodes, nodes), F32)
    count = out_ref.shape[0]
    stack = [gl_ref[i] for i in range(count - n)] + grids
    parts = []
    for i in range(count):
        parts.append(mm_hi(pick, run))
        run = run + stack[i]
    csend_s[...] = jnp.zeros_like(csend_s)
    csend_s[:, :nodes] = mm_hi(pick, run)
    copies = []
    for d in range(1, tilts):
        copies.append(pltpu.make_async_remote_copy(
            src_ref=csend_s, dst_ref=cslots.at[place],
            send_sem=csem.at[d - 1], recv_sem=crsem.at[d - 1],
            device_id={"tilt": lax.rem(place + d, tilts)}))
    for cp in copies:
        cp.start()
    cslots[place] = csend_s[...]
    for cp in copies:
        cp.wait()
    before = jnp.zeros((send_rows, 128), F32)
    for k in range(tilts):
        before = before + jnp.where(k < place, cslots[k], 0.0)
    for i in range(count):
        out_ref[i] = (before[:, :nodes] + parts[i])[:share]


def shards(images, taps, shifts, patch_rows, patch_cols, rows_interp, cols_interp):
    tilt_count, rows, cols = images.shape
    tiles, tilts = lax.axis_size("tile"), lax.axis_size("tilt")
    nodes = cols_interp.shape[0]
    patches = patch_rows.shape[1]
    first_rows = rows - CHUNK + MARGIN
    piece_a = images[0, :first_rows]
    piece_b = images[0, first_rows:]
    piece_a, piece_b, held = lax.optimization_barrier((piece_a, piece_b, images))
    next_a = shifted(piece_a, "tilt", -1)
    next_b = shifted(piece_b, "tilt", -1)
    low = shifted(held[:, rows - MARGIN :, :], "tile", 1)
    high = shifted(held[:, :MARGIN, :], "tile", -1)
    rim = shifted(jnp.concatenate([low[0], high[0]], axis=0), "tilt", -1)

    t_global = lax.axis_index("tilt") * tilt_count + jnp.arange(tilt_count, dtype=jnp.int32)
    valid = (t_global < tilt_count * tilts - 1).astype(jnp.int32)
    head = jnp.stack([lax.axis_index("tile") * rows, jnp.int32(rows * tiles)]).astype(jnp.int32)
    info = jnp.concatenate([head, jnp.concatenate([valid[:, None], shifts], axis=1).reshape(-1)])

    def halves(x):
        hi = lax.reduce_precision(x, 8, 7)
        return hi.astype(BF16), (x - hi).astype(BF16)

    chunks = rows // CHUNK
    rh, rl = halves(rows_interp.reshape(nodes, chunks, CHUNK).transpose(1, 0, 2))
    rcat = jnp.concatenate([rh, rh, rl], axis=2)
    ch, cl = halves(cols_interp)
    ccat = jnp.concatenate([ch, cl, ch], axis=0)
    eye = jnp.eye(nodes, dtype=F32)
    sel = jnp.concatenate([eye, eye, eye], axis=1)

    smem = pl.BlockSpec(memory_space=pltpu.SMEM)
    vmem = pl.BlockSpec(memory_space=pltpu.VMEM)
    vm = 60 << 20

    def per(shape, off=0):
        return pl.BlockSpec((1,) + shape, lambda i: (i + off, 0, 0))

    def whole(shape):
        return pl.BlockSpec(shape, lambda i: (0,) * len(shape))

    bands = [pltpu.VMEM((2 * WIDE, WIDE), BF16)] * 2
    e_scratch = pltpu.VMEM((rows + 2 * MARGIN, cols), F32)
    big = rows * cols
    w, w2, left_f = pl.pallas_call(
        k1,
        grid=(tilt_count,),
        in_specs=[smem, smem, per((1, patches)), per((patches, 1)), per((MARGIN, cols)),
                  per((rows, cols)), per((MARGIN, cols)), whole(rcat.shape)],
        out_specs=[per((rows, cols)), per((rows, cols)), per((nodes, cols))],
        out_shape=[jax.ShapeDtypeStruct((tilt_count, rows, cols), F32),
                   jax.ShapeDtypeStruct((tilt_count, rows, cols), F32),
                   jax.ShapeDtypeStruct((tilt_count, nodes, cols), F32)],
        scratch_shapes=[e_scratch, pltpu.VMEM((CHUNK, cols), F32), pltpu.VMEM((CHUNK, cols), F32),
                        pltpu.VMEM((CHUNK, cols), F32), pltpu.VMEM((patches, cols), BF16)] + bands,
        compiler_params=pltpu.CompilerParams(vmem_limit_bytes=vm),
        cost_estimate=pl.CostEstimate(flops=60 * big * tilt_count, bytes_accessed=40 * big * tilt_count,
                                      transcendentals=0),
        name="weigh",
    )(taps, info, patch_rows[:, None, :], patch_cols[:, :, None], low, images, high, rcat)

    def partner(pieces, first, count, off, start):
        taken = sum(p.shape[1] for p in pieces)
        area = (taken - 2 * MARGIN) * cols
        return pl.pallas_call(
            functools.partial(k2, first=first, pieces=len(pieces), start=start),
            grid=(count,),
            in_specs=[smem, smem] + [per(p.shape[1:], off) for p in pieces]
            + [whole(rcat.shape), per((rows, cols), first)],
            out_specs=per((nodes, cols)),
            out_shape=jax.ShapeDtypeStruct((count, nodes, cols), F32),
            scratch_shapes=[pltpu.VMEM((taken, cols), F32)] + bands,
            compiler_params=pltpu.CompilerParams(vmem_limit_bytes=vm),
            cost_estimate=pl.CostEstimate(flops=40 * area * count, bytes_accessed=30 * area * count,
                                          transcendentals=0),
            name="partner",
        )(taps, info, *pieces, rcat, w)

    rt = rows_interp.T

    def step(lq, lf, w2s, final, cid, extra=()):
        n = lq.shape[0]
        scratch = [pltpu.VMEM((nodes, cols), F32), pltpu.VMEM((rows, 3 * nodes), BF16),
                   pltpu.VMEM((CHUNK, COLB), F32), pltpu.VMEM((3 * n, nodes + 8, 128), F32),
                   pltpu.VMEM((3 * n, tiles, nodes + 8, 128), F32)]
        sems = [pltpu.SemaphoreType.DMA((3 * n, tiles - 1)), pltpu.SemaphoreType.DMA((3 * n, tiles - 1))]
        if final:
            share = nodes // tiles
            wide = max(8, share)
            scratch += [pltpu.VMEM((wide, 128), F32), pltpu.VMEM((tilts, wide, 128), F32)]
            sems += [pltpu.SemaphoreType.DMA((tilts - 1,)), pltpu.SemaphoreType.DMA((tilts - 1,))]
            out = jax.ShapeDtypeStruct((tilt_count, share, nodes), F32)
        else:
            out = jax.ShapeDtypeStruct((n, nodes, nodes), F32)
        off = tilt_count - 1 if final else 0
        args = (lq, lf, w2s, cols_interp, ccat, rt, rcat, sel) + tuple(extra)
        specs = [whole(lq.shape), pl.BlockSpec((n,) + lf.shape[1:], lambda i: (off, 0, 0)),
                 pl.BlockSpec((n,) + w2s.shape[1:], lambda i: (off, 0, 0))]
        specs += [whole(a.shape) for a in args[3:]]
        return pl.pallas_call(
            functools.partial(refine, n=n, final=final, sizes=(tiles, tilts)),
            grid=(1,),
            in_specs=specs,
            out_specs=pl.BlockSpec(out.shape, lambda i: (0, 0, 0)),
            out_shape=out,
            scratch_shapes=scratch + sems,
            compiler_params=pltpu.CompilerParams(
                collective_id=cid, has_side_effects=True, vmem_limit_bytes=vm),
            cost_estimate=pl.CostEstimate(flops=60 * big, bytes_accessed=40 * big, transcendentals=0),
            name="refine_last" if final else "refine_local",
        )(*args)

    local = tilt_count - 1
    extra = ()
    if local:
        lq = partner((low, images, high), 0, local, 1, 0)
        extra = (step(lq, left_f, w2, False, 1),)
    else:
        extra = (jnp.zeros((1, nodes, nodes), F32),)
    last = tilt_count - 1
    tail = first_rows - 2 * MARGIN
    lq_a = partner((rim[None, :MARGIN], next_a[None]), last, 1, 0, 0)
    lq_b = partner((next_a[None, tail:], next_b[None], rim[None, MARGIN:]), last, 1, 0, first_rows - MARGIN)
    return step(lq_a + lq_b, left_f, w2, True, 2, extra)


def solution(mesh):
    return jax.shard_map(
        shards,
        mesh=mesh,
        in_specs=(
            P("tilt", "tile", None),
            P(),
            P("tilt", None),
            P("tilt", None),
            P("tilt", None),
            P(None, "tile"),
            P(),
        ),
        out_specs=P("tilt", "tile", None),
        check_vma=False,
    )
```

```python
import functools

import jax
import jax.numpy as jnp
from jax import lax
from jax.experimental import pallas as pl
from jax.experimental.pallas import tpu as pltpu
from jax.sharding import PartitionSpec as P


RAD = 4
SMAX = 4
PATCH_HALF = 256
MARGIN = RAD + SMAX
CHUNK = 64
COLB = 512
WIDE = 256
GROUP = 32
PAD = 128
epsilon = 1e-06
F32 = jnp.float32
BF16 = jnp.bfloat16
HI = lax.Precision.HIGHEST


def shifted(value, axis, steps):
    count = lax.axis_size(axis)
    initial, last = (max(0, -steps), min(count, count - steps))
    return lax.ppermute(value, axis, [(source, source + steps) for source in range(initial, last)])


def split_rows(x):
    hi = x.astype(BF16)
    lo = (x - hi.astype(F32)).astype(BF16)
    return jnp.concatenate([hi, lo, hi], axis=0)


def mm(a, b):
    return jnp.dot(a, b, preferred_element_type=F32)


def mm_hi(a, b):
    return lax.dot_general(
        a, b, (((1,), (0,)), ((), ())), precision=HI, preferred_element_type=F32
    )


def toeplitz(taps_ref, dx, th_s, tl_s):
    i = lax.broadcasted_iota(jnp.int32, (2 * WIDE, WIDE), 0)
    o = lax.broadcasted_iota(jnp.int32, (2 * WIDE, WIDE), 1)
    rel = jnp.where(i < WIDE, i, jnp.where(i < WIDE + PAD, i - WIDE - PAD, i - PAD))
    d = rel - o - dx + RAD
    t = jnp.zeros((2 * WIDE, WIDE), F32)
    for k in range(2 * RAD + 1):
        t = jnp.where(d == k, taps_ref[k], t)
    th_s[...], tl_s[...] = split3(t)


def filter_group(load, store, rows, cols, dx, th_s, tl_s):
    blocks = cols // PAD
    zero = jnp.zeros((rows, PAD), BF16)
    his, los = [zero], [zero]
    for b in range(blocks):
        hi, lo = split3(load(b * PAD, PAD))
        his.append(hi)
        los.append(lo)
    his.append(zero)
    los.append(zero)

    def gather(v):
        return jnp.concatenate(
            [jnp.concatenate([v[2 * b + 1], v[2 * b + 2], v[2 * b], v[2 * b + 3]], axis=1)
             for b in range(blocks // 2)], axis=0)

    xh, xl = gather(his), gather(los)
    th = th_s[...]
    e = mm(xh, th) + (mm(xl, th) + mm(xh, tl_s[...]))
    for b in range(blocks // 2):
        v = e[b * rows : (b + 1) * rows]
        if b == 0 or b == blocks // 2 - 1:
            x = lax.broadcasted_iota(jnp.int32, v.shape, 1) + (b * WIDE + dx)
            v = jnp.where((x >= 0) & (x < cols), v, 0.0)
        store(b * WIDE, v)


def filter_pieces(pieces, e_s, cols, dx, th_s, tl_s):
    at = 0
    for ref in pieces:
        m = ref.shape[1]
        groups = m // GROUP

        def body(i, carry, ref=ref, at=at):
            r = pl.multiple_of(i * GROUP, 8)
            ro = pl.multiple_of(i * GROUP + at, 8)

            def load(c, w):
                return ref[0, pl.ds(r, GROUP), c : c + w]

            def store(c, v):
                e_s[pl.ds(ro, GROUP), c : c + WIDE] = v

            filter_group(load, store, GROUP, cols, dx, th_s, tl_s)
            return carry

        if groups:
            lax.fori_loop(0, groups, body, 0)
        done = groups * GROUP
        left = m - done
        while left:
            size = 16 if left >= 16 else 8

            def load(c, w, ref=ref, done=done, size=size):
                return ref[0, done : done + size, c : c + w]

            def store(c, v, at=at, done=done, size=size):
                e_s[at + done : at + done + size, c : c + WIDE] = v

            filter_group(load, store, size, cols, dx, th_s, tl_s)
            done += size
            left -= size
        at += m


def band(taps_ref, dy):
    ext = CHUNK + 2 * MARGIN
    y = lax.broadcasted_iota(jnp.int32, (CHUNK, 3 * ext), 0)
    j = lax.broadcasted_iota(jnp.int32, (CHUNK, 3 * ext), 1)
    j = jnp.where(j >= 2 * ext, j - 2 * ext, jnp.where(j >= ext, j - ext, j))
    d = j - y - (MARGIN - RAD) - dy
    out = jnp.zeros((CHUNK, 3 * ext), F32)
    for k in range(2 * RAD + 1):
        out = jnp.where(d == k, taps_ref[k], out)
    return out


def stacked(m):
    hi, lo = split3(m)
    lane = lax.broadcasted_iota(jnp.int32, m.shape, 1)
    return jnp.where(lane < 2 * m.shape[1] // 3, hi.astype(F32), lo.astype(F32)).astype(BF16)


def split3(m):
    hi = m.astype(BF16)
    lo = (m - hi.astype(F32)).astype(BF16)
    return hi, lo


def k1(taps_ref, info_ref, prow_ref, pcol_ref, up_ref, main_ref, down_ref, rcat_ref,
       w_ref, w2_ref, left_ref, e_s, f_s, m_s, p_s, cb_s, th_s, tl_s):
    rows, cols = main_ref.shape[1:]
    t = pl.program_id(0)
    band_start = info_ref[0]
    valid = info_ref[2 + 3 * t].astype(F32)
    toeplitz(taps_ref, 0, th_s, tl_s)
    filter_pieces((up_ref, main_ref, down_ref), e_s, cols, 0, th_s, tl_s)
    left_ref[...] = jnp.zeros_like(left_ref)
    patches = prow_ref.shape[2]
    xcol = lax.broadcasted_iota(jnp.int32, (patches, cols), 1)
    cb_s[...] = (jnp.abs(xcol - pcol_ref[0]) <= PATCH_HALF).astype(F32).astype(BF16)
    tm = stacked(band(taps_ref, 0))

    def chunk(c, carry):
        base = pl.multiple_of(c * CHUNK, CHUNK)
        yrow = band_start + base + lax.broadcasted_iota(jnp.int32, (CHUNK, patches), 0)
        rb = ((jnp.abs(yrow - prow_ref[0]) <= PATCH_HALF).astype(F32) * valid).astype(BF16)
        for b in range(cols // COLB):
            cs = slice(b * COLB, (b + 1) * COLB)
            e = e_s[pl.ds(base, CHUNK + 2 * MARGIN), cs]
            f_s[:, cs] = mm(tm, split_rows(e))
            m_s[:, cs] = mm(rb, cb_s[:, cs])

        def weigh(i, cc):
            r = pl.multiple_of(i * 8, 8)
            f = f_s[pl.ds(r, 8), :]
            fp = jnp.concatenate([f, jnp.zeros((8, PAD), F32)], axis=1)
            wd = cols + PAD
            gx = 0.5 * (pltpu.roll(fp, wd - 1, 1) - pltpu.roll(fp, 1, 1))[:, :cols]
            w = m_s[pl.ds(r, 8), :] * gx
            ro = pl.multiple_of(base + r, 8)
            w_ref[0, pl.ds(ro, 8), :] = w
            w2_ref[0, pl.ds(ro, 8), :] = w * gx
            p_s[pl.ds(r, 8), :] = -(w * f)
            return cc

        lax.fori_loop(0, CHUNK // 8, weigh, 0)
        rc = rcat_ref[c]
        for b in range(cols // COLB):
            cs = slice(b * COLB, (b + 1) * COLB)
            left_ref[0, :, cs] += mm(rc, split_rows(p_s[:, cs]))
        return carry

    lax.fori_loop(0, rows // CHUNK, chunk, 0)


def k2(taps_ref, info_ref, *refs, first, pieces, start):
    piece_refs = refs[:pieces]
    rcat_ref, w_ref, init_ref, left_ref, e_s, th_s, tl_s = refs[pieces:]
    rows = sum(p.shape[1] for p in piece_refs) - 2 * MARGIN
    cols = w_ref.shape[2]
    t = pl.program_id(0) + first
    band_start = info_ref[0] + start
    total_rows = info_ref[1]
    dy = info_ref[3 + 3 * t]
    dx = info_ref[4 + 3 * t]
    toeplitz(taps_ref, dx, th_s, tl_s)
    filter_pieces(piece_refs, e_s, cols, dx, th_s, tl_s)
    left_ref[...] = init_ref[...]
    tm = band(taps_ref, dy)
    yl = lax.broadcasted_iota(jnp.int32, tm.shape, 0) + band_start + dy

    def chunk(c, carry):
        base = pl.multiple_of(c * CHUNK, CHUNK)
        y = yl + base
        tc = stacked(jnp.where((y >= 0) & (y < total_rows), tm, 0.0))
        rc = rcat_ref[c + start // CHUNK]
        for b in range(cols // COLB):
            cs = slice(b * COLB, (b + 1) * COLB)
            q = mm(tc, split_rows(e_s[pl.ds(base, CHUNK + 2 * MARGIN), cs]))
            p = w_ref[0, pl.ds(pl.multiple_of(base + start, CHUNK), CHUNK), cs] * q
            left_ref[0, :, cs] += mm(rc, split_rows(p))
        return carry

    lax.fori_loop(0, rows // CHUNK, chunk, 0)


def refine(*refs, n, final, sizes):
    if final:
        (lq_ref, w2_ref, ccat_ref, rt_ref, r2_ref, sel_ref, gl_ref, out_ref,
         left_s, cat_s, acc_s, send_s, slots, csend_s, cslots, ssem, rsem, csem, crsem) = refs
    else:
        (lq_ref, w2_ref, ccat_ref, rt_ref, r2_ref, sel_ref, out_ref,
         left_s, cat_s, acc_s, send_s, slots, ssem, rsem) = refs
    tiles, tilts = sizes
    nodes, cols = lq_ref.shape[1:]
    rows = rt_ref.shape[0]
    me = lax.axis_index("tile")
    place = lax.axis_index("tilt")
    barrier = pltpu.get_barrier_semaphore()
    for d in range(1, tiles):
        pl.semaphore_signal(barrier, inc=1, device_id={"tile": lax.rem(me + d, tiles)})
    waits = tiles - 1
    if final:
        for d in range(1, tilts):
            pl.semaphore_signal(barrier, inc=1, device_id={"tilt": lax.rem(place + d, tilts)})
        waits += tilts - 1
    pl.semaphore_wait(barrier, waits)

    def exchange(rnd):
        copies = []
        for d in range(1, tiles):
            copies.append(pltpu.make_async_remote_copy(
                src_ref=send_s.at[rnd], dst_ref=slots.at[rnd, me],
                send_sem=ssem.at[rnd, d - 1], recv_sem=rsem.at[rnd, d - 1],
                device_id={"tile": lax.rem(me + d, tiles)}))
        for cp in copies:
            cp.start()
        slots[rnd, me] = send_s[rnd]
        for cp in copies:
            cp.wait()
        total = slots[rnd, 0]
        for k in range(1, tiles):
            total = total + slots[rnd, k]
        return total

    def project(left):
        hi, lo = split3(left)
        q = lax.dot_general(jnp.concatenate([hi, lo], axis=0), ccat_ref[: 2 * nodes, :],
                            (((1,), (1,)), ((), ())), preferred_element_type=F32)
        q = q[:nodes] + q[nodes:]
        return (q + pltpu.roll(q, nodes, 1))[:, :nodes]

    def direction(g, w2, apply):
        cat_s[...] = stacked(mm_hi(rt_ref[...], mm_hi(g, sel_ref[...])))
        acc_s[...] = jnp.zeros_like(acc_s)

        def block(b, carry):
            cs = pl.ds(pl.multiple_of(b * COLB, COLB), COLB)
            v = mm(cat_s[...], ccat_ref[:, cs])
            y = w2_ref[w2, :, cs] * v
            acc_s[...] += jnp.sum((y * v).reshape(rows // 8, 8, COLB), axis=0)
            if apply:
                yh, yl = split3(y)
                top = mm(r2_ref[...], yh)
                left_s[:, cs] = top[:nodes] + (top[nodes:] + mm(r2_ref[:nodes, :], yl))
            return carry

        lax.fori_loop(0, cols // COLB, block, 0)
        return jnp.sum(acc_s[...])

    grids = []
    for s in range(n):
        r = 3 * s
        send_s[r] = jnp.zeros_like(send_s[r])
        send_s[r, :nodes, :nodes] = project(lq_ref[s])
        g1 = exchange(r)[:nodes, :nodes]
        gg1 = jnp.sum(g1 * g1)
        jj1 = direction(g1, s, True)
        send_s[r + 1] = jnp.zeros_like(send_s[r + 1])
        send_s[r + 1, :nodes, :nodes] = project(left_s[...])
        send_s[r + 1, nodes : nodes + 8, :] = jnp.full((8, send_s.shape[2]), jj1, F32)
        both = exchange(r + 1)
        h1 = both[:nodes, :nodes]
        jj1 = jnp.sum(both[nodes : nodes + 1, 0:1])
        a1 = jnp.full((nodes, nodes), gg1, F32) / jnp.full((nodes, nodes), jj1 + epsilon, F32)
        g2 = g1 - a1 * h1
        gg2 = jnp.sum(g2 * g2)
        jj2 = direction(g2, s, False)
        send_s[r + 2] = jnp.full(send_s.shape[1:], jj2, F32)
        jj2 = jnp.sum(exchange(r + 2)[0:1, 0:1])
        a2 = jnp.full((nodes, nodes), gg2, F32) / jnp.full((nodes, nodes), jj2 + epsilon, F32)
        grids.append(-(a1 * g1) - a2 * g2)
    if not final:
        for s in range(n):
            out_ref[s] = grids[s]
        return
    share = nodes // tiles
    send_rows = csend_s.shape[0]
    row = lax.broadcasted_iota(jnp.int32, (send_rows, nodes), 0) + me * share
    pick = (row == lax.broadcasted_iota(jnp.int32, (send_rows, nodes), 1)).astype(F32)
    run = jnp.zeros((nodes, nodes), F32)
    count = out_ref.shape[0]
    stack = [gl_ref[i] for i in range(count - n)] + grids
    parts = []
    for i in range(count):
        parts.append(mm_hi(pick, run))
        run = run + stack[i]
    csend_s[...] = jnp.zeros_like(csend_s)
    csend_s[:, :nodes] = mm_hi(pick, run)
    copies = []
    for d in range(1, tilts):
        copies.append(pltpu.make_async_remote_copy(
            src_ref=csend_s, dst_ref=cslots.at[place],
            send_sem=csem.at[d - 1], recv_sem=crsem.at[d - 1],
            device_id={"tilt": lax.rem(place + d, tilts)}))
    for cp in copies:
        cp.start()
    cslots[place] = csend_s[...]
    for cp in copies:
        cp.wait()
    before = jnp.zeros((send_rows, 128), F32)
    for k in range(tilts):
        before = before + jnp.where(k < place, cslots[k], 0.0)
    for i in range(count):
        out_ref[i] = (before[:, :nodes] + parts[i])[:share]


def shards(images, taps, shifts, patch_rows, patch_cols, rows_interp, cols_interp):
    tilt_count, rows, cols = images.shape
    tiles, tilts = lax.axis_size("tile"), lax.axis_size("tilt")
    nodes = cols_interp.shape[0]
    patches = patch_rows.shape[1]
    first_rows = rows - CHUNK + MARGIN
    piece_a = images[0, :first_rows]
    piece_b = images[0, first_rows:]
    piece_a, piece_b, held = lax.optimization_barrier((piece_a, piece_b, images))
    next_a = shifted(piece_a, "tilt", -1)
    low = shifted(held[:, rows - MARGIN :, :], "tile", 1)
    high = shifted(held[:, :MARGIN, :], "tile", -1)
    rim = shifted(jnp.concatenate([low[0], high[0]], axis=0), "tilt", -1)
    next_b = shifted(piece_b, "tilt", -1)

    t_global = lax.axis_index("tilt") * tilt_count + jnp.arange(tilt_count, dtype=jnp.int32)
    valid = (t_global < tilt_count * tilts - 1).astype(jnp.int32)
    head = jnp.stack([lax.axis_index("tile") * rows, jnp.int32(rows * tiles)]).astype(jnp.int32)
    info = jnp.concatenate([head, jnp.concatenate([valid[:, None], shifts], axis=1).reshape(-1)])

    def halves(x):
        hi = lax.reduce_precision(x, 8, 7)
        return hi.astype(BF16), (x - hi).astype(BF16)

    chunks = rows // CHUNK
    rh, rl = halves(rows_interp.reshape(nodes, chunks, CHUNK).transpose(1, 0, 2))
    rcat = jnp.concatenate([rh, rh, rl], axis=2)
    ch, cl = halves(cols_interp)
    ccat = jnp.concatenate([ch, cl, ch], axis=0)
    eye = jnp.eye(nodes, dtype=F32)
    sel = jnp.concatenate([eye, eye, eye], axis=1)

    smem = pl.BlockSpec(memory_space=pltpu.SMEM)
    vmem = pl.BlockSpec(memory_space=pltpu.VMEM)
    vm = 60 << 20

    def per(shape, off=0):
        return pl.BlockSpec((1,) + shape, lambda i: (i + off, 0, 0))

    def whole(shape):
        return pl.BlockSpec(shape, lambda i: (0,) * len(shape))

    bands = [pltpu.VMEM((2 * WIDE, WIDE), BF16)] * 2
    e_scratch = pltpu.VMEM((rows + 2 * MARGIN, cols), F32)
    big = rows * cols
    w, w2, left_f = pl.pallas_call(
        k1,
        grid=(tilt_count,),
        in_specs=[smem, smem, per((1, patches)), per((patches, 1)), per((MARGIN, cols)),
                  per((rows, cols)), per((MARGIN, cols)), whole(rcat.shape)],
        out_specs=[per((rows, cols)), per((rows, cols)), per((nodes, cols))],
        out_shape=[jax.ShapeDtypeStruct((tilt_count, rows, cols), F32),
                   jax.ShapeDtypeStruct((tilt_count, rows, cols), F32),
                   jax.ShapeDtypeStruct((tilt_count, nodes, cols), F32)],
        scratch_shapes=[e_scratch, pltpu.VMEM((CHUNK, cols), F32), pltpu.VMEM((CHUNK, cols), F32),
                        pltpu.VMEM((CHUNK, cols), F32), pltpu.VMEM((patches, cols), BF16)] + bands,
        compiler_params=pltpu.CompilerParams(vmem_limit_bytes=vm),
        cost_estimate=pl.CostEstimate(flops=60 * big * tilt_count, bytes_accessed=40 * big * tilt_count,
                                      transcendentals=0),
        name="weigh",
    )(taps, info, patch_rows[:, None, :], patch_cols[:, :, None], low, images, high, rcat)

    def partner(pieces, init, at, first, count, off, start):
        taken = sum(p.shape[1] for p in pieces)
        area = (taken - 2 * MARGIN) * cols
        return pl.pallas_call(
            functools.partial(k2, first=first, pieces=len(pieces), start=start),
            grid=(count,),
            in_specs=[smem, smem] + [per(p.shape[1:], off) for p in pieces]
            + [whole(rcat.shape), per((rows, cols), first), per((nodes, cols), at)],
            out_specs=per((nodes, cols)),
            out_shape=jax.ShapeDtypeStruct((count, nodes, cols), F32),
            scratch_shapes=[pltpu.VMEM((taken, cols), F32)] + bands,
            compiler_params=pltpu.CompilerParams(vmem_limit_bytes=vm),
            cost_estimate=pl.CostEstimate(flops=40 * area * count, bytes_accessed=30 * area * count,
                                          transcendentals=0),
            name="partner",
        )(taps, info, *pieces, rcat, w, init)

    rt = rows_interp.T
    gh, gl = halves(rows_interp)
    r2 = jnp.concatenate([gh, gl], axis=0)

    def step(lq, w2s, final, cid, extra=()):
        n = lq.shape[0]
        scratch = [pltpu.VMEM((nodes, cols), F32), pltpu.VMEM((rows, 3 * nodes), BF16),
                   pltpu.VMEM((8, COLB), F32), pltpu.VMEM((3 * n, nodes + 8, 128), F32),
                   pltpu.VMEM((3 * n, tiles, nodes + 8, 128), F32)]
        sems = [pltpu.SemaphoreType.DMA((3 * n, tiles - 1)), pltpu.SemaphoreType.DMA((3 * n, tiles - 1))]
        if final:
            share = nodes // tiles
            wide = max(8, share)
            scratch += [pltpu.VMEM((wide, 128), F32), pltpu.VMEM((tilts, wide, 128), F32)]
            sems += [pltpu.SemaphoreType.DMA((tilts - 1,)), pltpu.SemaphoreType.DMA((tilts - 1,))]
            out = jax.ShapeDtypeStruct((tilt_count, share, nodes), F32)
        else:
            out = jax.ShapeDtypeStruct((n, nodes, nodes), F32)
        off = tilt_count - 1 if final else 0
        args = (lq, w2s, ccat, rt, r2, sel) + tuple(extra)
        specs = [whole(lq.shape), pl.BlockSpec((n,) + w2s.shape[1:], lambda i: (off, 0, 0))]
        specs += [whole(a.shape) for a in args[2:]]
        return pl.pallas_call(
            functools.partial(refine, n=n, final=final, sizes=(tiles, tilts)),
            grid=(1,),
            in_specs=specs,
            out_specs=pl.BlockSpec(out.shape, lambda i: (0, 0, 0)),
            out_shape=out,
            scratch_shapes=scratch + sems,
            compiler_params=pltpu.CompilerParams(
                collective_id=cid, has_side_effects=True, vmem_limit_bytes=vm),
            cost_estimate=pl.CostEstimate(flops=60 * big, bytes_accessed=40 * big, transcendentals=0),
            name="refine_last" if final else "refine_local",
        )(*args)

    local = tilt_count - 1
    extra = ()
    if local:
        lq = partner((low, images, high), left_f, 0, 0, local, 1, 0)
        extra = (step(lq, w2, False, 1),)
    else:
        extra = (jnp.zeros((1, nodes, nodes), F32),)
    last = tilt_count - 1
    tail = first_rows - 2 * MARGIN
    lq_a = partner((rim[None, :MARGIN], next_a[None]), left_f, last, last, 1, 0, 0)
    lq_b = partner((next_a[None, tail:], next_b[None], rim[None, MARGIN:]), lq_a, 0, last, 1, 0,
                   first_rows - MARGIN)
    return step(lq_b, w2, True, 2, extra)


def solution(mesh):
    return jax.shard_map(
        shards,
        mesh=mesh,
        in_specs=(
            P("tilt", "tile", None),
            P(),
            P("tilt", None),
            P("tilt", None),
            P("tilt", None),
            P(None, "tile"),
            P(),
        ),
        out_specs=P("tilt", "tile", None),
        check_vma=False,
    )
```
